32 devices in a mesh: rep: 16 (over z, y, core), shard: 2 (over x).
Axes of the slice: x: 2, y: 2, z: 4, core: 2. Of those that a mesh axis runs over, the one named last changes fastest.
Arguments:
- tokens: bfloat16 [16384, 1024], P(('rep', 'shard')), may hold values from -120 to 120
- cotangent: bfloat16 [16384, 1024], P(('rep', 'shard')), may hold values from -6 to 6
- qkv_weight: bfloat16 [1024, 3072], P('shard'), may hold values from -0.1875 to 0.1875
- query_bias: bfloat16 [1024], P('shard'), may hold values from -3 to 3
- value_bias: bfloat16 [1024], P('shard'), may hold values from -3 to 3
- proj_weight: bfloat16 [1024, 1024], P('shard'), may hold values from -2 to 2
- proj_bias: bfloat16 [1024], P('shard'), may hold values from -3 to 3
- norm1_gain: bfloat16 [1024], P('shard'), may hold values from 0.099609375 to 1.8984375
- norm1_shift: bfloat16 [1024], P('shard'), may hold values from -3 to 3
- norm2_gain: bfloat16 [1024], P('shard'), may hold values from 0.099609375 to 1.8984375
- norm2_shift: bfloat16 [1024], P('shard'), may hold values from -3 to 3
- fc1_weight: bfloat16 [1024, 4096], P('shard'), may hold values from -0.1875 to 0.1875
- fc1_bias: bfloat16 [4096], P('shard'), may hold values from -3 to 3
- fc2_weight: bfloat16 [4096, 1024], P('shard'), may hold values from -0.09375 to 0.09375
- fc2_bias: bfloat16 [1024], P('shard'), may hold values from -3 to 3
Outputs:
- result: float32 [16384, 1024], P(('rep', 'shard'))
- input_grad: float32 [16384, 1024], P(('rep', 'shard'))
- qkv_weight_grad: float32 [1024, 3072], P('shard')
- query_bias_grad: float32 [1024], P('shard')
- value_bias_grad: float32 [1024], P('shard')
- proj_weight_grad: float32 [1024, 1024], P('shard')
- proj_bias_grad: float32 [1024], P('shard')
- norm1_gain_grad: float32 [1024], P('shard')
- norm1_shift_grad: float32 [1024], P('shard')
- norm2_gain_grad: float32 [1024], P('shard')
- norm2_shift_grad: float32 [1024], P('shard')
- fc1_weight_grad: float32 [1024, 4096], P('shard')
- fc1_bias_grad: float32 [4096], P('shard')
- fc2_weight_grad: float32 [4096, 1024], P('shard')
- fc2_bias_grad: float32 [1024], P('shard')
- rms_input: float32 [], replicated
- rms_middle: float32 [], replicated
- rms_output: float32 [], replicated
The draws below stay inside these ranges and needn't reach their ends.
All inputs are finite; a program needn't handle non-finite values.
Results may differ from the reference program's by a relative error of at most 0.012.
The reference program's roundings to bfloat16 on the way count: a program that leaves them out, or rounds other values in their place, can miss the bound.
Values may be sent and summed in bfloat16 or wider, within the bound.
No kernel may reach another device: no remote copies, remote signals or barrier semaphores. Data moves between devices by JAX's collectives and lax.ppermute only.
A program may use at most 256 MiB of HBM per device.

```python
import math
import jax
import jax.numpy as jnp
from jax import lax

D = 1024
H = 16
HD = 64
FF = 4096
SEQ = 512
TOKENS = 16384


def draw_tokens(key, part):
    first_key, second_key = jax.random.split(jax.random.fold_in(key, 17))
    clip_index = jnp.arange(TOKENS) // SEQ
    clip_total = TOKENS // SEQ
    rising = clip_index.astype(jnp.float32) / max(clip_total - 1, 1)
    row_scale = 10.0 ** rising
    column_scale = jnp.exp(jax.random.uniform(second_key, (D,), minval=0.0, maxval=math.log(3.0)))
    base_values = jax.random.truncated_normal(first_key, -4.0, 4.0, (TOKENS, D))
    return (base_values * row_scale[:, None] * column_scale[None, :]).astype(jnp.bfloat16)


def raised(drawn, key, source, target, blocks, factor):
    owner, partner = [(jnp.arange(drawn.shape[position]) // (drawn.shape[position] // blocks)).reshape([-1 if axis == position else 1 for axis in range(drawn.ndim)]) for position in (source, target)]
    chosen = jax.random.permutation(key, blocks)[partner]
    strong = (owner == chosen) | (owner == (partner + blocks // 2) % blocks)
    return jnp.where(strong, factor * drawn, drawn)


def level_of(own_key, dims, cuts, least, top_value):
    level = 1.0
    for axis_at, shards_of in cuts:
        steps = jax.random.uniform(jax.random.fold_in(jax.random.fold_in(own_key, 6), axis_at), (shards_of,), jnp.float32, least / len(cuts), top_value / len(cuts))
        level = level * jnp.repeat(jnp.exp(steps), dims[axis_at] // shards_of).reshape((-1,) + (1,) * (len(dims) - 1 - axis_at))
    return level


def scatter_about(own_key, dims, scale, limit, cuts=(), dtype=jnp.bfloat16):
    entries = jax.random.normal(own_key, dims, jnp.float32) * scale
    if len(cuts) > 0:
        entries = level_of(own_key, dims, cuts, -0.22, 0.18) * entries
    return jnp.clip(entries, min=-limit, max=limit).astype(dtype)


def bell_draw_with(own_key, dims, deviation, most, cuts, heavy, dtype=jnp.bfloat16):
    drawn = deviation * jax.random.normal(own_key, dims, jnp.float32)
    if cuts:
        drawn = drawn * level_of(own_key, dims, cuts, -0.22, 0.18)
    return jnp.clip(raised(drawn, jax.random.fold_in(own_key, 3), *heavy), -most, most).astype(dtype)


def setup_inputs(seed: int = 0) -> dict:
    seeds = jax.random.split(jax.random.key(seed), 16)
    return {
        "tokens": draw_tokens(jax.random.fold_in(seeds[15], 71), 0),
        "cotangent": bell_draw_with(seeds[1], (TOKENS, D), 1.0, 6.0, ((0, 32),), (0, 1, 32, 2.75)),
        "qkv_weight": scatter_about(seeds[2], (D, 3 * D), D ** -0.5, 0.1875, ((0, 2),)),
        "query_bias": scatter_about(seeds[3], (D,), 0.5, 3.0, ((0, 2),)),
        "value_bias": scatter_about(seeds[4], (D,), 0.5, 3.0, ((0, 2),)),
        "proj_weight": scatter_about(seeds[5], (D, D), (D * 4 // SEQ) ** -0.5, 2.0, ((0, 2),)),
        "proj_bias": scatter_about(seeds[6], (D,), 0.5, 3.0, ((0, 2),)),
        "norm1_gain": jnp.clip(1.0 + 0.18 * jax.random.normal(seeds[7], (D,), jnp.float32), 0.099609375, 1.8984375).astype(jnp.bfloat16),
        "norm1_shift": scatter_about(seeds[8], (D,), 0.5, 3.0, ((0, 2),)),
        "norm2_gain": jnp.clip(1.0 + 0.18 * jax.random.normal(seeds[9], (D,), jnp.float32), 0.099609375, 1.8984375).astype(jnp.bfloat16),
        "norm2_shift": scatter_about(seeds[10], (D,), 0.5, 3.0, ((0, 2),)),
        "fc1_weight": scatter_about(seeds[11], (D, FF), D ** -0.5, 0.1875, ((0, 2),)),
        "fc1_bias": scatter_about(seeds[12], (FF,), 0.5, 3.0, ((0, 2),)),
        "fc2_weight": scatter_about(seeds[13], (FF, D), FF ** -0.5, 0.09375, ((0, 2),)),
        "fc2_bias": scatter_about(seeds[14], (D,), 0.5, 3.0, ((0, 2),)),
    }


@jax.custom_vjp
def low(v):
    return lax.optimization_barrier(v.astype(jnp.bfloat16)).astype(jnp.float32)

@jax.custom_vjp
def low_back(v):
    return v

def low_keep(v):
    return (low(v), None)

def low_pass(kept, grad):
    return (grad,)

def back_keep(v):
    return (v, None)

def back_low(kept, grad):
    return (low(grad),)
low.defvjp(low_keep, low_pass)
low_back.defvjp(back_keep, back_low)

def matmul_high(left, right):
    return jnp.dot(left, right, precision=lax.Precision.HIGHEST, preferred_element_type=jnp.float32)

def normalize(values, gain, shift):
    centre = values - lax.optimization_barrier(jnp.mean(values, axis=1, keepdims=True))
    spread = lax.optimization_barrier(jnp.mean(centre * centre, axis=1, keepdims=True))
    return centre * lax.rsqrt(spread + 1e-05) * gain + shift

def exact_gelu(values):
    return jax.nn.gelu(values, approximate=False)

def clip_attention(parts):
    query_clip, key_clip, value_clip = parts
    query_heads = query_clip.reshape(SEQ, H, HD)
    key_heads = key_clip.reshape(SEQ, H, HD)
    value_heads = value_clip.reshape(SEQ, H, HD)
    scores = low_back(jnp.einsum('qhd,khd->hqk', query_heads, key_heads, precision=lax.Precision.HIGHEST) * 0.125)
    attn_probs = low(jax.nn.softmax(scores, axis=-1))
    mixed = jnp.einsum('hqk,khd->qhd', attn_probs, value_heads, precision=lax.Precision.HIGHEST)
    return mixed.reshape(SEQ, H * HD)

def forward(inputs, weights):
    attn_in, bias_query, bias_value, attn_out, bias_attn, gain_first, shift_first, gain_second, shift_second, mlp_in, bias_hidden, mlp_out, bias_output = weights
    normed_one = low(normalize(inputs, gain_first, shift_first))
    projected = matmul_high(normed_one, attn_in)
    queries = low_back(low(projected[:, :D] + bias_query))
    keys_all = low_back(low(projected[:, D:2 * D]))
    values_all = low_back(low(projected[:, 2 * D:] + bias_value))
    clip_count = inputs.shape[0] // SEQ
    mixed = lax.map(jax.checkpoint(clip_attention), (queries.reshape(clip_count, SEQ, D), keys_all.reshape(clip_count, SEQ, D), values_all.reshape(clip_count, SEQ, D)))
    mixed = low_back(low(mixed.reshape(clip_count * SEQ, D)))
    attended = low_back(matmul_high(mixed, attn_out) + bias_attn)
    middle = inputs + attended
    normed_two = low(normalize(middle, gain_second, shift_second))
    hidden_pre = low_back(matmul_high(normed_two, mlp_in) + bias_hidden)
    hidden_act = low(exact_gelu(hidden_pre))
    result = middle + low_back(matmul_high(hidden_act, mlp_out) + bias_output)
    return (result, middle)

def root_mean(values):
    return jnp.sqrt(jnp.sum(values * values) / (TOKENS * D) + 1e-06)

def reference(tokens, cotangent, qkv_weight, query_bias, value_bias, proj_weight, proj_bias, norm1_gain, norm1_shift, norm2_gain, norm2_shift, fc1_weight, fc1_bias, fc2_weight, fc2_bias):
    inputs = tokens.astype(jnp.float32)
    weights = tuple((leaf_value.astype(jnp.float32) for leaf_value in (qkv_weight, query_bias, value_bias, proj_weight, proj_bias, norm1_gain, norm1_shift, norm2_gain, norm2_shift, fc1_weight, fc1_bias, fc2_weight, fc2_bias)))
    result, pullback, middle = jax.vjp(forward, inputs, weights, has_aux=True)
    input_grad, weight_grads = pullback(cotangent.astype(jnp.float32))
    factor = 1.0 / math.sqrt(TOKENS)
    scaled = tuple((leaf_value * factor for leaf_value in weight_grads))
    return (result, input_grad, scaled[0], scaled[1], scaled[2], scaled[3], scaled[4], scaled[5], scaled[6], scaled[7], scaled[8], scaled[9], scaled[10], scaled[11], scaled[12], root_mean(inputs), root_mean(middle), root_mean(result))
```

```python
import functools
import math

import jax
import jax.numpy as jnp
from jax import lax
from jax.experimental import pallas as pl
from jax.experimental.pallas import tpu as pltpu
from jax.sharding import PartitionSpec as P


HD = 64
BF = jnp.bfloat16
F32 = jnp.float32
VMEM_LIMIT = 48 << 20


def dot(left, right, left_dim, right_dim):
    return lax.dot_general(
        left, right, (((left_dim,), (right_dim,)), ((), ())), preferred_element_type=F32
    )


def column_sum(values):
    return jnp.sum(values.astype(F32), axis=0)


def attend_forward_kernel(q_ref, k_ref, v_ref, o_ref, lse_ref):
    outs = []
    for h in range(2):
        cols = slice(h * HD, (h + 1) * HD)
        query = q_ref[:, cols] * BF(0.125)
        scores = dot(k_ref[:, cols], query, 1, 1)
        top = jnp.max(scores, axis=0, keepdims=True)
        powers = jnp.exp(scores - top)
        total = jnp.sum(powers, axis=0, keepdims=True)
        probs = (powers * (1.0 / total)).astype(BF)
        outs.append(dot(v_ref[:, cols], probs, 0, 0).T.astype(BF))
        lse_ref[0, h : h + 1, :] = top + jnp.log(total)
    o_ref[...] = jnp.concatenate(outs, axis=1)


def attend_forward(projected):
    rows, width = projected.shape[0], projected.shape[1] // 3
    pairs = width // 128

    def part(offset):
        return pl.BlockSpec((rows, 128), lambda i: (0, i + offset))

    return pl.pallas_call(
        attend_forward_kernel,
        grid=(pairs,),
        in_specs=[part(0), part(pairs), part(2 * pairs)],
        out_specs=[part(0), pl.BlockSpec((1, 2, rows), lambda i: (i, 0, 0))],
        out_shape=[
            jax.ShapeDtypeStruct((rows, width), BF),
            jax.ShapeDtypeStruct((pairs, 2, rows), F32),
        ],
        compiler_params=pltpu.CompilerParams(vmem_limit_bytes=VMEM_LIMIT),
        cost_estimate=pl.CostEstimate(
            flops=16 * rows * rows * width, bytes_accessed=8 * rows * width, transcendentals=0
        ),
    )(projected, projected, projected)


def attend_backward_kernel(pairs, core_ref, q_ref, k_ref, v_ref, d_ref, lse_ref, send_ref, keep_ref):
    step = pl.program_id(0)
    half = pairs // 2
    parts = [[], [], []]
    for h in range(2):
        cols = slice(h * HD, (h + 1) * HD)
        query = q_ref[:, cols] * BF(0.125)
        key, value, grad = k_ref[:, cols], v_ref[:, cols], d_ref[:, cols]
        exact = jnp.exp(dot(key, query, 1, 1) - lse_ref[0, h : h + 1, :])
        weighted = exact * dot(value, grad, 1, 1)
        inner = jnp.sum(weighted, axis=0, keepdims=True)
        grad_scores = (weighted - exact * inner).astype(BF)
        parts[2].append(dot(exact.astype(BF), grad, 1, 0).astype(BF))
        parts[1].append(dot(grad_scores, query, 1, 0).astype(BF))
        parts[0].append((dot(key, grad_scores, 0, 0) * 0.125).T.astype(BF))
    blocks = [jnp.concatenate(part, axis=1) for part in parts]

    def store(ref):
        for at, block in enumerate(blocks):
            start = pl.multiple_of((at * half + lax.rem(step, half)) * 128, 128)
            ref[:, pl.ds(start, 128)] = block

    pl.when(step < half)(lambda: store(send_ref))
    pl.when(step >= half)(lambda: store(keep_ref))


def attend_backward(projected, grad_out, lse, core):
    rows, width = grad_out.shape
    pairs = width // 128
    half = pairs // 2

    def pair(i, core_ref):
        first = 1 - core_ref[0]
        return jnp.where(i < half, first, 1 - first) * half + lax.rem(i, half)

    def part(offset):
        return pl.BlockSpec((rows, 128), lambda i, c: (0, pair(i, c) + offset))

    whole = pl.BlockSpec((rows, 3 * width // 2), lambda i, c: (0, 0))
    return pl.pallas_call(
        functools.partial(attend_backward_kernel, pairs),
        grid_spec=pltpu.PrefetchScalarGridSpec(
            num_scalar_prefetch=1,
            grid=(pairs,),
            in_specs=[
                part(0),
                part(pairs),
                part(2 * pairs),
                part(0),
                pl.BlockSpec((1, 2, rows), lambda i, c: (pair(i, c), 0, 0)),
            ],
            out_specs=[whole, whole],
        ),
        out_shape=[jax.ShapeDtypeStruct((rows, 3 * width // 2), BF)] * 2,
        compiler_params=pltpu.CompilerParams(vmem_limit_bytes=VMEM_LIMIT),
        cost_estimate=pl.CostEstimate(
            flops=40 * rows * rows * width, bytes_accessed=14 * rows * width, transcendentals=0
        ),
    )(core.reshape(1), projected, projected, projected, grad_out, lse)


def place_kernel(order, index_ref, *refs):
    out_ref = refs[-1]
    step = pl.program_id(0)
    for at in range(len(order)):

        @pl.when(step == at)
        def _(at=at):
            out_ref[...] = refs[order[at]][...].astype(out_ref.dtype)


def place(pieces, targets):
    rows = min(piece.shape[0] for piece in pieces)
    width = pieces[0].shape[1]
    order, inner = [], []
    for at, piece in enumerate(pieces):
        for block in range(piece.shape[0] // rows):
            order.append(at)
            inner.append(block)
    steps = len(order)
    views = [piece.reshape(-1, rows, width) for piece in pieces]
    specs = []
    for at, view in enumerate(views):
        first = order.index(at)
        last = view.shape[0] - 1
        specs.append(
            pl.BlockSpec(
                (1, rows, width),
                lambda i, t, first=first, last=last: (jnp.clip(i - first, 0, last), 0, 0),
            )
        )
    out = pl.pallas_call(
        functools.partial(place_kernel, order),
        grid_spec=pltpu.PrefetchScalarGridSpec(
            num_scalar_prefetch=1,
            grid=(steps,),
            in_specs=specs,
            out_specs=pl.BlockSpec((1, rows, width), lambda i, t: (t[i], 0, 0)),
        ),
        out_shape=jax.ShapeDtypeStruct((steps, rows, width), BF),
        compiler_params=pltpu.CompilerParams(vmem_limit_bytes=VMEM_LIMIT),
        cost_estimate=pl.CostEstimate(
            flops=0, bytes_accessed=4 * steps * rows * width, transcendentals=0
        ),
    )(targets, *views)
    return out.reshape(steps * rows, width)


def spread_kernel(index_ref, a_ref, b_ref, c_ref, d_ref, out_ref):
    for at, ref in enumerate((a_ref, b_ref, c_ref, d_ref)):

        @pl.when(pl.program_id(0) * 2 + pl.program_id(1) == at)
        def _(ref=ref):
            out_ref[...] = ref[...].astype(F32)


def spread(quarters, row_bit, column_bit, groups):
    rows, width = quarters[0].shape
    columns = width // groups
    specs = []
    for at in range(4):

        def index(i, j, g, t, at=at):
            now = i * 2 + j
            return (0, jnp.where(now < at, 0, jnp.where(now > at, groups - 1, g)))

        specs.append(pl.BlockSpec((rows, columns), index))
    return pl.pallas_call(
        spread_kernel,
        grid_spec=pltpu.PrefetchScalarGridSpec(
            num_scalar_prefetch=1,
            grid=(2, 2, groups),
            in_specs=specs,
            out_specs=pl.BlockSpec(
                (rows, columns),
                lambda i, j, g, t: (lax.bitwise_xor(i, t[0]), g * 2 + lax.bitwise_xor(j, t[1])),
            ),
        ),
        out_shape=jax.ShapeDtypeStruct((2 * rows, 2 * width), F32),
        compiler_params=pltpu.CompilerParams(vmem_limit_bytes=VMEM_LIMIT),
        cost_estimate=pl.CostEstimate(
            flops=0, bytes_accessed=24 * rows * width, transcendentals=0
        ),
    )(jnp.stack([row_bit, column_bit]), *quarters)


class Place:
    def __init__(self):
        self.reps = lax.axis_size("rep")
        self.shards = lax.axis_size("shard")
        self.levels = self.reps // 4
        rep = lax.axis_index("rep")
        self.core = lax.bitwise_and(rep, 1)
        self.y = lax.bitwise_and(lax.shift_right_logical(rep, 1), 1)
        self.z = lax.shift_right_logical(rep, 2)
        self.x = lax.axis_index("shard")

    def rep_swap(self, values, mask):
        return lax.ppermute(values, "rep", [(i, i ^ mask) for i in range(self.reps)])

    def to_core(self, values):
        return self.rep_swap(values, 1)

    def to_y(self, values):
        return self.rep_swap(values, 2)

    def to_z(self, values, distance):
        return self.rep_swap(values, 4 * distance)

    def to_x(self, values):
        return lax.ppermute(values, "shard", [(0, 1), (1, 0)])


def gather_rows(place_at, own):
    if place_at.shards != 2:
        return lax.all_gather(own, "shard", axis=0, tiled=True)
    rows = own.shape[0] // 4
    mine = place_at.y * 2 + place_at.core
    first = place_at.to_x(lax.dynamic_slice_in_dim(own, mine * rows, rows, 0))
    second = place_at.to_y(first)
    third, fourth = place_at.to_core(first), place_at.to_core(second)
    base = (1 - place_at.x) * 4
    targets = [place_at.x * 4 + i for i in range(4)] + [
        base + lax.bitwise_xor(mine, flip) for flip in (0, 2, 1, 3)
    ]
    return place([own, first, second, third, fourth], jnp.stack(targets))


def reduce_weight(at, left, left_sibling, right, right_sibling, factor, groups=1):
    total_rows = left.shape[1]
    share = total_rows // at.shards
    quarter = share // 2

    def partial(start, rows):
        return dot(
            lax.dynamic_slice_in_dim(left, start, rows, 1), right, 0, 0
        ) + dot(lax.dynamic_slice_in_dim(left_sibling, start, rows, 1), right_sibling, 0, 0)

    if at.shards == 2:
        other, own = (1 - at.x) * share, at.x * share
        away, home = (1 - at.y) * quarter, at.y * quarter
        first = at.to_x(partial(other + away, quarter).astype(BF))
        second = at.to_x(partial(other + home, quarter).astype(BF))
        outgoing = (partial(own + away, quarter) + first.astype(F32)).astype(BF)
        kept = partial(own + home, quarter) + second.astype(F32)
    else:
        mine = lax.psum_scatter(
            partial(0, total_rows).astype(BF), "shard", scatter_dimension=0, tiled=True
        )
        outgoing = lax.dynamic_slice_in_dim(mine, (1 - at.y) * quarter, quarter, 0)
        kept = lax.dynamic_slice_in_dim(mine, at.y * quarter, quarter, 0).astype(F32)
    kept = kept + at.to_y(outgoing).astype(F32)
    rows = quarter // at.levels
    total = lax.dynamic_slice_in_dim(kept, at.z * rows, rows, 0)
    for distance in range(1, at.levels):
        target = lax.bitwise_xor(at.z, distance)
        piece = lax.dynamic_slice_in_dim(kept, target * rows, rows, 0).astype(BF)
        total = total + at.to_z(piece, distance).astype(F32)
    total = (total * factor).astype(BF)
    pieces = [total] + [at.to_z(total, distance) for distance in range(1, at.levels)]
    targets = jnp.stack([lax.bitwise_xor(at.z, distance) for distance in range(at.levels)])
    near = place(pieces, targets)
    far = at.to_y(near)
    return spread(
        [near, at.to_core(near), far, at.to_core(far)], at.y, at.core, groups
    )


def reduce_vectors(at, values):
    for mask in [1 << bit for bit in range(at.reps.bit_length() - 1)]:
        values = values + at.rep_swap(values, mask)
    if at.shards == 2:
        return values + at.to_x(values)
    return lax.psum(values, "shard")


def normalized(values):
    centre = values - jnp.mean(values, axis=1, keepdims=True)
    scale = lax.rsqrt(jnp.mean(centre * centre, axis=1, keepdims=True) + 1e-05)
    return centre * scale, scale


def normalize_back(grad, hat, scale, gain):
    scaled = grad * gain
    return scale * (
        scaled
        - jnp.mean(scaled, axis=1, keepdims=True)
        - hat * jnp.mean(scaled * hat, axis=1, keepdims=True)
    )


def gelu_parts(values):
    below = 0.5 * (1.0 + lax.erf(values * (1.0 / math.sqrt(2.0))))
    density = jnp.exp(values * values * -0.5) * (1.0 / math.sqrt(2.0 * math.pi))
    return values * below, below + values * density


def on_device(
    tokens,
    cotangent,
    qkv_weight,
    query_bias,
    value_bias,
    proj_weight,
    proj_bias,
    norm1_gain,
    norm1_shift,
    norm2_gain,
    norm2_shift,
    fc1_weight,
    fc1_bias,
    fc2_weight,
    fc2_bias,
):
    at = Place()
    row_count, width = tokens.shape
    token_total = at.reps * at.shards * row_count
    factor = 1.0 / math.sqrt(token_total)

    small = (
        query_bias,
        value_bias,
        proj_bias,
        norm1_gain,
        norm1_shift,
        norm2_gain,
        norm2_shift,
        fc1_bias,
        fc2_bias,
    )
    packed = jnp.concatenate(small)
    if at.shards == 2:
        arrived = at.to_x(packed)
        packed = jnp.stack(
            [jnp.where(at.x == 0, packed, arrived), jnp.where(at.x == 0, arrived, packed)]
        )
    else:
        packed = lax.all_gather(packed, "shard", axis=0)
    full, start = [], 0
    for vector in small:
        full.append(packed[:, start : start + vector.shape[0]].reshape(-1).astype(F32))
        start += vector.shape[0]
    (
        bias_query,
        bias_value,
        bias_attn,
        gain_first,
        shift_first,
        gain_second,
        shift_second,
        bias_hidden,
        bias_output,
    ) = full

    attn_in = gather_rows(at, qkv_weight)
    attn_out = gather_rows(at, proj_weight)
    mlp_in = gather_rows(at, fc1_weight)
    mlp_out = gather_rows(at, fc2_weight)

    def halves(values):
        size = values.shape[1] // 2
        keep = lax.dynamic_slice_in_dim(values, at.core * size, size, 1)
        send = lax.dynamic_slice_in_dim(values, (1 - at.core) * size, size, 1)
        return keep, at.to_core(send)

    inputs = tokens.astype(F32)
    hat_first, scale_first = normalized(inputs)
    normed_one = (hat_first * gain_first + shift_first).astype(BF)
    normed_one_sibling = at.to_core(normed_one)
    cot_keep, cot_sibling = halves(cotangent)
    bias_projected = jnp.concatenate([bias_query, jnp.zeros_like(bias_query), bias_value])
    projected = (dot(normed_one, attn_in, 1, 0) + bias_projected).astype(BF)
    mixed, lse = attend_forward(projected)
    mixed_sibling = at.to_core(mixed)
    middle = inputs + (dot(mixed, attn_out, 1, 0) + bias_attn)
    hat_second, scale_second = normalized(middle)
    normed_two = (hat_second * gain_second + shift_second).astype(BF)
    normed_two_sibling = at.to_core(normed_two)
    hidden_pre = dot(normed_two, mlp_in, 1, 0) + bias_hidden
    hidden_act, slope = gelu_parts(hidden_pre)
    hidden_act = hidden_act.astype(BF)
    hidden_sibling = at.to_core(hidden_act)
    result = middle + (dot(hidden_act, mlp_out, 1, 0) + bias_output)

    grad_mlp_out = reduce_weight(
        at, hidden_act, hidden_sibling, cot_keep, cot_sibling, factor
    )
    grad_pre = (dot(cotangent, mlp_out, 1, 1) * slope).astype(BF)
    pre_keep, pre_sibling = halves(grad_pre)
    grad_mlp_in = reduce_weight(
        at, normed_two, normed_two_sibling, pre_keep, pre_sibling, factor
    )
    grad_normed_two = dot(grad_pre, mlp_in, 1, 1)
    grad_gain_second = jnp.sum(grad_normed_two * hat_second, axis=0)
    grad_shift_second = jnp.sum(grad_normed_two, axis=0)
    grad_middle = cotangent.astype(F32) + normalize_back(
        grad_normed_two, hat_second, scale_second, gain_second
    )
    grad_attended = grad_middle.astype(BF)
    attended_keep, attended_sibling = halves(grad_attended)
    grad_attn_out = reduce_weight(
        at, mixed, mixed_sibling, attended_keep, attended_sibling, factor
    )
    grad_mixed = dot(grad_attended, attn_out, 1, 1).astype(BF)
    projected_send, projected_keep = attend_backward(projected, grad_mixed, lse, at.core)
    projected_sibling = at.to_core(projected_send)
    grad_attn_in = reduce_weight(
        at, normed_one, normed_one_sibling, projected_keep, projected_sibling, factor, groups=3
    )
    low = jnp.where(at.core == 0, projected_keep, projected_send)
    high = jnp.where(at.core == 0, projected_send, projected_keep)
    half = width // 2
    grad_projected = jnp.concatenate(
        [part[:, i * half : (i + 1) * half] for i in range(3) for part in (low, high)], axis=1
    )
    grad_normed_one = dot(grad_projected, attn_in, 1, 1)
    grad_gain_first = jnp.sum(grad_normed_one * hat_first, axis=0)
    grad_shift_first = jnp.sum(grad_normed_one, axis=0)
    input_grad = grad_middle + normalize_back(
        grad_normed_one, hat_first, scale_first, gain_first
    )

    squares = jnp.stack(
        [jnp.sum(inputs * inputs), jnp.sum(middle * middle), jnp.sum(result * result)]
    )
    sums_projected = column_sum(grad_projected)
    vectors = [
        sums_projected[:width],
        sums_projected[2 * width :],
        column_sum(grad_attended),
        grad_gain_first,
        grad_shift_first,
        grad_gain_second,
        grad_shift_second,
        column_sum(grad_pre),
        column_sum(cotangent),
    ]
    summed = reduce_vectors(
        at, jnp.concatenate(vectors + [squares, jnp.zeros((125,), F32)])
    )
    owned, start = [], 0
    for vector in vectors:
        size = vector.shape[0] // at.shards
        owned.append(
            lax.dynamic_slice_in_dim(summed, start + at.x * size, size, 0) * factor
        )
        start += vector.shape[0]
    root_means = jnp.sqrt(summed[start : start + 3] / (token_total * width) + 1e-06)
    return (
        result,
        input_grad,
        grad_attn_in,
        owned[0],
        owned[1],
        grad_attn_out,
        owned[2],
        owned[3],
        owned[4],
        owned[5],
        owned[6],
        grad_mlp_in,
        owned[7],
        grad_mlp_out,
        owned[8],
        root_means[0],
        root_means[1],
        root_means[2],
    )


def solution(mesh):
    split, rows, vector = P(("rep", "shard"), None), P("shard", None), P("shard")
    in_specs = (
        split,
        split,
        rows,
        vector,
        vector,
        rows,
        vector,
        vector,
        vector,
        vector,
        vector,
        rows,
        vector,
        rows,
        vector,
    )
    out_specs = (split, split) + in_specs[2:] + (P(), P(), P())
    return jax.shard_map(
        on_device, mesh=mesh, in_specs=in_specs, out_specs=out_specs, check_vma=False
    )
```
